128 devices in a mesh: tile: 32 (over z, y, core), frame: 4 (over x).
Axes of the slice: x: 4, y: 4, z: 4, core: 2. Of those that a mesh axis runs over, the one named last changes fastest.
Arguments:
- movie: bfloat16 [128, 2048, 256], P(('frame', 'tile')), may hold values from -6 to 6
- footprints: bfloat16 [2048, 256, 384], P('tile'), may hold values from -0.09375 to 0.09375
- support: int32 [256, 384], P('tile'), may hold values 0 or 1
- traces: bfloat16 [12288, 128], P('tile', 'frame'), may hold values from 0 to 2
- border_weight: float32 [2048, 256], P('tile'), may hold values from 1 to 4
- border_offsets: int32 [64, 2], replicated, may hold values from -16 to 16, as said below
Outputs:
- new_traces: float32 [12288, 128], P('tile', 'frame')
- trace_gram: float32 [12288, 384], P('tile')
- remainder: bfloat16 [128, 2048, 256], P(('frame', 'tile'))
The draws below stay inside these ranges and needn't reach their ends.
Inputs may be any that keep to these rules, and one draw needn't show every extreme that they name: `border_offsets`: the 64 rows are distinct offsets (row, column) on the boundary of the square of half-side 16; (-16, -16) and (16, 16) are among them.
All inputs are finite; a program needn't handle non-finite values. No bound on the sum of `support` on one device may be relied on, other than what follows from the above.
Results may differ from the reference program's by a relative error of at most 0.009.
Values may be sent and summed in bfloat16 or wider, within the bound.
A program may use at most 128 MiB of HBM per device.

```python
import math
import jax
import jax.numpy as jnp
import numpy as np
from jax import lax

TH = 64
W = 256
KT = 384
RR = 16
GR = 4
BR = 8
SWEEPS = 3
NR = 64
H = 2048
K = 12288
FRAMES = 128
N_TILE = 32


def draw_border_offsets(key, part):
    perimeter = 8 * RR
    remaining = np.concatenate([np.arange(1, 4 * RR), np.arange(4 * RR + 1, perimeter)]).astype(np.int32)
    shuffled = jax.random.permutation(key, perimeter - 2)
    chosen = jnp.concatenate([jnp.array([0, 4 * RR], jnp.int32), jnp.asarray(remaining)[shuffled[:NR - 2]]])
    which_side = chosen // (2 * RR)
    position = chosen % (2 * RR) - RR
    offset_rows = jnp.where(which_side == 0, -RR, jnp.where(which_side == 1, position, jnp.where(which_side == 2, RR, -position)))
    offset_cols = jnp.where(which_side == 0, position, jnp.where(which_side == 1, RR, jnp.where(which_side == 2, -position, -RR)))
    return jnp.stack([offset_rows, offset_cols], axis=1).astype(jnp.int32)


def set_ends(values, rng, least, top_value):
    longest = values.shape.index(max(values.shape))
    spots = []
    for shift in (0, 1):
        where = [jax.random.randint(jax.random.fold_in(rng, axis), (), 0, length) for axis, length in enumerate(values.shape)]
        where[longest] = (where[longest] + shift) % values.shape[longest]
        spots.append(tuple(where))
    return values.at[spots[0]].set(least).at[spots[1]].set(top_value)


def block_scale(own_key, dims, split, smallest, high):
    def one(axis_at, parts):
        heights = jax.random.uniform(jax.random.fold_in(jax.random.fold_in(own_key, 6), axis_at), (parts,), jnp.float32, smallest / len(split), high / len(split))
        return jnp.repeat(jnp.exp(heights), dims[axis_at] // parts).reshape((-1,) + (1,) * (len(dims) - axis_at - 1))

    loudness = one(*split[0])
    for cut in split[1:]:
        loudness = loudness * one(*cut)
    return loudness


def gaussian(own_key, shape, scale, bound, shards=(), kind=jnp.bfloat16):
    factor_of = block_scale(own_key, shape, shards, -0.22, 0.18) if shards else 1.0
    result = jax.random.normal(own_key, shape, jnp.float32) * scale * factor_of
    return jnp.minimum(jnp.maximum(result, -bound), bound).astype(kind)


def setup_inputs(seed: int = 0) -> dict:
    streams_of = jax.random.split(jax.random.key(seed), 7)
    movie = gaussian(streams_of[0], (FRAMES, H, W), 1.0, 6.0, ((0, 128),))
    footprints = gaussian(streams_of[1], (H, W, KT), (TH * W // 4) ** -0.5, 0.09375, ((0, 32),))
    support = set_ends((jax.random.randint(streams_of[2], (H // BR, KT), 0, 2) < 1).astype(jnp.int32), jax.random.fold_in(streams_of[2], 1), 0, 1)
    traces = jnp.clip(2.0 * jax.random.uniform(streams_of[3], (K, FRAMES), jnp.float32) ** block_scale(streams_of[3], (K, FRAMES), ((0, 32), (1, 4)), -0.2, 0.2), 0.0, 2.0).astype(jnp.bfloat16)
    border_weight = jnp.clip(jnp.exp(math.log(4.0) - 1.3862944 * jax.random.uniform(streams_of[4], (H, W), jnp.float32) ** block_scale(streams_of[4], (H, W), ((0, 32),), -0.2, 0.2)), 1.0, 4.0)
    border_offsets = draw_border_offsets(jax.random.fold_in(streams_of[6], 71), 0)
    return dict(movie=movie, footprints=footprints, support=support, traces=traces, border_weight=border_weight, border_offsets=border_offsets)


def gaussian_taps(radius):
    spots = jnp.arange(-radius, radius + 1).astype(jnp.float32)
    raw_weights = jnp.exp(-2.0 * spots * spots / float(radius * radius))
    return raw_weights / jnp.sum(raw_weights)

def smooth_along(values_in, taps_table, radius, along_axis):
    extent = values_in.shape[along_axis]
    pad_widths = [(0, 0)] * values_in.ndim
    pad_widths[along_axis] = (radius, radius)
    padded = jnp.pad(values_in, pad_widths)
    running = jnp.zeros(values_in.shape, jnp.float32)
    for offset_step in range(2 * radius + 1):
        running = running + taps_table[offset_step] * lax.slice_in_dim(padded, offset_step, offset_step + extent, axis=along_axis)
    return running

def reference(movie, footprints, support, traces, border_weight, border_offsets):
    frames_all = movie.shape[0]
    pixel_count = TH * W
    block_masks = jnp.repeat(support, BR, axis=0).astype(jnp.bfloat16)
    shaped = (footprints * block_masks[:, None, :]).reshape(N_TILE, pixel_count, KT)
    grouped = traces.reshape(N_TILE, KT, frames_all)
    pixels = movie.reshape(frames_all, N_TILE, pixel_count).transpose(1, 0, 2)

    def activity(operands):
        strip_fp, strip_tr = operands
        return jnp.einsum('kf,pk->fp', strip_tr, strip_fp, preferred_element_type=jnp.float32)
    fitted = lax.map(activity, (shaped, grouped))
    first = (pixels.astype(jnp.float32) - fitted).astype(jnp.bfloat16)
    image = first.transpose(1, 0, 2).reshape(frames_all, H, W)
    taps_table = gaussian_taps(GR)
    smooth = smooth_along(smooth_along(image.astype(jnp.float32), taps_table, GR, 1), taps_table, GR, 2).astype(jnp.bfloat16)
    padded = jnp.pad(smooth.astype(jnp.float32), ((0, 0), (RR, RR), (RR, RR)))
    zero_index = jnp.zeros((), jnp.int32)

    def add_offset(offset_step, running):
        row_start = (border_offsets[offset_step, 0] + RR).astype(jnp.int32)
        col_start = (border_offsets[offset_step, 1] + RR).astype(jnp.int32)
        return running + lax.dynamic_slice(padded, (zero_index, row_start, col_start), (frames_all, H, W))
    summed = lax.fori_loop(0, NR, add_offset, jnp.zeros((frames_all, H, W), jnp.float32))
    background = border_weight[None, :, :] * summed / math.sqrt(NR)
    cleaned = (movie.astype(jnp.float32) - background).astype(jnp.bfloat16)
    cleaned_strips = cleaned.reshape(frames_all, N_TILE, pixel_count).transpose(1, 0, 2)

    def temporal(operands):
        strip_fp, strip_tr, strip_data = operands
        projected = jnp.einsum('pk,fp->kf', strip_fp, strip_data, preferred_element_type=jnp.float32)
        coupling = jnp.einsum('pk,pq->kq', strip_fp, strip_fp, preferred_element_type=jnp.float32)
        floor_t = jnp.maximum(jnp.diagonal(coupling), 1.0)
        trace_state = strip_tr.astype(jnp.float32)
        for sweep_index in range(SWEEPS):
            moved = jnp.dot(coupling, trace_state, precision=lax.Precision.HIGHEST)
            trace_state = jnp.maximum(trace_state + (projected - moved) / floor_t[:, None], 0.0)
        gram_block = jnp.dot(trace_state, trace_state.T, precision=lax.Precision.HIGHEST)
        rounded = trace_state.astype(jnp.bfloat16)
        refit = jnp.einsum('kf,pk->fp', rounded, strip_fp, preferred_element_type=jnp.float32)
        leftover = (strip_data.astype(jnp.float32) - refit).astype(jnp.bfloat16)
        return (trace_state, gram_block, leftover)
    new_traces, trace_gram, leftover = lax.map(temporal, (shaped, grouped, cleaned_strips))
    remainder = leftover.transpose(1, 0, 2).reshape(frames_all, H, W)
    return (new_traces.reshape(N_TILE * KT, frames_all), trace_gram.reshape(N_TILE * KT, KT), remainder)
```

```python
import functools
import math

import jax
import jax.numpy as jnp
import numpy as np
from jax import lax
from jax.experimental import pallas as pl
from jax.experimental.pallas import tpu as pltpu
from jax.sharding import PartitionSpec as P

RR = 16
GR = 4
BR = 8
SWEEPS = 3
NR = 64
TH = 64
W = 256
KT = 384
HB = 32
NBLOCK = TH // BR
CHUNKS = 4
CROWS = TH // CHUNKS
F32 = jnp.float32
BF16 = jnp.bfloat16

_raw = np.exp(-2.0 * np.arange(-GR, GR + 1, dtype=np.float32) ** 2 / np.float32(GR * GR)).astype(np.float32)
TAPS = _raw / _raw.sum(dtype=np.float32)


def tap(d):
    away = jnp.abs(d)
    value = jnp.zeros(d.shape, F32)
    for step in range(GR + 1):
        value = jnp.where(away == step, float(TAPS[GR + step]), value)
    return value


def dot(a, b):
    return jnp.dot(a, b, preferred_element_type=F32)


def dot_nt(a, b):
    return lax.dot_general(a, b, (((1,), (1,)), ((), ())), preferred_element_type=F32)


def dot_tn(a, b):
    return lax.dot_general(a, b, (((0,), (0,)), ((), ())), preferred_element_type=F32)


def split(a):
    high = a.astype(BF16)
    return high, (a - high.astype(F32)).astype(BF16)


def build_operators(me, tiles, offs, rmat, cmat):
    rows_of, cols_of = offs[0:1, :], offs[1:2, :]
    place = lax.broadcasted_iota(jnp.int32, (128, NR), 0) - RR
    col_hot = (place == cols_of).astype(F32)
    row_hot = (place == rows_of).astype(F32)
    inner = jnp.abs(rows_of) < RR
    which = lax.broadcasted_iota(jnp.int32, (8, NR), 0)
    side_rows = jnp.where(which == 0, rows_of, jnp.where(which == 1, rows_of, 99))
    is_row = ((which == 0) & (side_rows == -RR)) | ((which == 1) & (side_rows == RR))
    is_col = inner & (((which == 0) & (cols_of == -RR)) | ((which == 1) & (cols_of == RR)))
    row_sides = dot_nt(is_row.astype(F32), col_hot)
    col_sides = dot_nt(is_col.astype(F32), row_hot)

    u = lax.broadcasted_iota(jnp.int32, (W, W), 0)
    x = lax.broadcasted_iota(jnp.int32, (W, W), 1)
    gap = u - x
    smooth_high, smooth_low = split(tap(gap))
    for side in range(2):
        band = jnp.zeros((W, W), F32)
        for b in range(-RR, RR + 1):
            band = jnp.where(gap == b, row_sides[side : side + 1, b + RR : b + RR + 1], band)
        band = band.astype(BF16)
        cmat[side * W : (side + 1) * W, :] = (dot(smooth_high, band) + dot(smooth_low, band)).astype(BF16)
        shift = RR if side == 0 else -RR
        source = x - shift
        kept = (source >= 0) & (source < W)
        cmat[(2 + side) * W : (3 + side) * W, :] = jnp.where(kept, tap(u - source), 0.0).astype(BF16)

    total_rows = tiles * TH
    y = lax.broadcasted_iota(jnp.int32, (TH, 128), 0)
    v = lax.broadcasted_iota(jnp.int32, (TH, 128), 1)
    rel = jnp.where(v < TH, v, jnp.where(v < TH + HB, v - (TH + HB), v - HB))

    def inside(row):
        place_of = row + me * TH
        return (place_of >= 0) & (place_of < total_rows)

    seen = inside(rel)
    parts = []
    for a in (-RR, RR):
        parts.append(jnp.where(seen & inside(y + a), tap(rel - y - a), 0.0))
    left = jnp.zeros((TH, 128), F32)
    right = jnp.zeros((TH, 128), F32)
    for a in range(-RR + 1, RR):
        term = jnp.where(seen & inside(y + a), tap(rel - y - a), 0.0)
        left = left + term * col_sides[0:1, a + RR : a + RR + 1]
        right = right + term * col_sides[1:2, a + RR : a + RR + 1]
    for index, part in enumerate(parts + [left, right]):
        high, low = split(part)
        rmat[index * TH : (index + 1) * TH, 0:128] = high
        rmat[index * TH : (index + 1) * TH, 128:256] = low


def kernel(
    tiles, slabs, movie, foot, support, traces, weight, offs, out_traces, out_gram, out_rest,
    shaped, strips, flat, first, above, below, cmat, rmat, stage, cleaned, coupling, rest, gathered,
    load_sem, in_send, in_recv, halo_send, halo_recv, gram_send, gram_recv, out_send, out_recv,
):
    me = lax.axis_index("tile")
    slab = lax.axis_index("frame")
    frames = tiles
    group = min(8, frames)
    groups = frames // group

    barrier = pltpu.get_barrier_semaphore()

    @pl.loop(1, tiles)
    def _(step):
        pl.semaphore_signal(barrier, inc=1, device_id={"tile": lax.rem(me + step, tiles)})

    for step in range(1, slabs):
        pl.semaphore_signal(barrier, inc=1, device_id={"frame": lax.rem(slab + step, slabs)})

    for block in range(NBLOCK):
        span = pl.ds(block * BR, BR)
        pltpu.make_async_copy(foot.at[span], shaped.at[span], load_sem.at[block]).start()

    build_operators(me, tiles, offs, rmat, cmat)

    @pl.when(me == 0)
    def _():
        above[...] = jnp.zeros(above.shape, BF16)

    @pl.when(me == tiles - 1)
    def _():
        below[...] = jnp.zeros(below.shape, BF16)

    pl.semaphore_wait(barrier, tiles - 1 + slabs - 1)

    def movie_copy(peer):
        return pltpu.make_async_remote_copy(
            src_ref=movie.at[0, pl.ds(pl.multiple_of(peer * TH, TH), TH), :],
            dst_ref=strips.at[me],
            send_sem=in_send,
            recv_sem=in_recv.at[me],
            device_id={"tile": peer},
        )

    @pl.loop(1, tiles)
    def _(step):
        movie_copy(lax.rem(me + step, tiles)).start()

    pltpu.make_async_copy(
        movie.at[0, pl.ds(pl.multiple_of(me * TH, TH), TH), :], strips.at[me], in_recv.at[me]
    ).start()

    coupling[...] = jnp.zeros(coupling.shape, F32)
    old = traces[...]

    @pl.loop(0, NBLOCK)
    def _(block):
        span = pl.ds(block * BR, BR)
        pltpu.make_async_copy(foot.at[span], shaped.at[span], load_sem.at[block]).wait()
        mask = support[pl.ds(block, 1), :].astype(F32).astype(BF16)
        for inner in range(BR):
            row = block * BR + inner
            masked = shaped[row] * mask
            shaped[row] = masked
            fit = dot_nt(old, masked)
            at = pl.ds(pl.multiple_of(row * frames, frames), frames)
            flat[0, at, :] = fit[:, 0:128]
            flat[1, at, :] = fit[:, 128:256]
        pixels = shaped[span].reshape(BR * W, KT)
        coupling[...] += dot_tn(pixels, pixels)

    def halo_up(g):
        span = pl.ds(g * group, group)
        return pltpu.make_async_remote_copy(
            src_ref=first.at[span, pl.ds(0, HB), :],
            dst_ref=below.at[span],
            send_sem=halo_send.at[0, g],
            recv_sem=halo_recv.at[0, g],
            device_id={"tile": lax.max(me - 1, 0)},
        )

    def halo_down(g):
        span = pl.ds(g * group, group)
        return pltpu.make_async_remote_copy(
            src_ref=first.at[span, pl.ds(TH - HB, HB), :],
            dst_ref=above.at[span],
            send_sem=halo_send.at[1, g],
            recv_sem=halo_recv.at[1, g],
            device_id={"tile": lax.min(me + 1, tiles - 1)},
        )

    for g in range(groups):

        @pl.loop(0, group)
        def _(inner):
            f = g * group + inner
            pltpu.make_async_copy(strips.at[f], strips.at[f], in_recv.at[f]).wait()
            seen = strips[f].astype(F32)
            at = pl.ds(f, TH, stride=frames)
            first[f, :, 0:128] = (seen[:, 0:128] - flat[0, at, :]).astype(BF16)
            first[f, :, 128:256] = (seen[:, 128:256] - flat[1, at, :]).astype(BF16)

        @pl.when(me > 0)
        def _():
            halo_up(g).start()

        @pl.when(me < tiles - 1)
        def _():
            halo_down(g).start()

    for g in range(groups):

        @pl.when(me > 0)
        def _():
            halo_down(g).wait_recv()

        @pl.when(me < tiles - 1)
        def _():
            halo_up(g).wait_recv()

        @pl.loop(0, group)
        def _(inner):
            f = g * group + inner
            window = jnp.concatenate([first[f], above[f], below[f]], axis=0)
            filtered = dot(rmat[...], jnp.concatenate([window, window], axis=0))
            at = pl.ds(pl.multiple_of(inner * TH, TH), TH)
            for side in range(4):
                stage[at, side * W : (side + 1) * W] = filtered[side * TH : (side + 1) * TH].astype(BF16)

        ring = dot(stage[...], cmat[...])
        scale = weight[...] / math.sqrt(NR)
        for inner in range(group):
            f = g * group + inner
            clean = strips[f].astype(F32) - scale * ring[inner * TH : (inner + 1) * TH]
            clean = clean.astype(BF16).astype(F32)
            at = pl.ds(f, TH, stride=frames)
            cleaned[0, at, :] = clean[:, 0:128]
            cleaned[1, at, :] = clean[:, 128:256]

    def project(row, total):
        at = pl.ds(pl.multiple_of(row * frames, frames), frames)
        pixels = jnp.concatenate([cleaned[0, at, :], cleaned[1, at, :]], axis=1).astype(BF16)
        return total + dot(pixels, shaped[row])

    def project_block(block, total):
        for inner in range(BR):
            total = project(block * BR + inner, total)
        return total

    projected = lax.fori_loop(0, NBLOCK, project_block, jnp.zeros((frames, KT), F32))

    matrix = coupling[...]
    here = lax.broadcasted_iota(jnp.int32, (KT, KT), 0) == lax.broadcasted_iota(jnp.int32, (KT, KT), 1)
    floor = jnp.maximum(jnp.sum(jnp.where(here, matrix, 0.0), axis=0, keepdims=True), 1.0)
    matrix_high, matrix_low = split(matrix)
    state = old.astype(F32)
    for _ in range(SWEEPS):
        high, low = split(state)
        moved = dot(high, matrix_high) + (dot(high, matrix_low) + dot(low, matrix_high))
        state = jnp.maximum(state + (projected - moved) / floor, 0.0)
    out_traces[...] = state
    new = state.astype(BF16)
    gathered[slab] = new

    def gram_copy(peer):
        return pltpu.make_async_remote_copy(
            src_ref=gathered.at[slab],
            dst_ref=gathered.at[slab],
            send_sem=gram_send.at[peer],
            recv_sem=gram_recv.at[slab],
            device_id={"frame": peer},
        )

    for step in range(1, slabs):
        gram_copy(lax.rem(slab + step, slabs)).start()

    def rest_copy(peer, chunk):
        return pltpu.make_async_remote_copy(
            src_ref=rest.at[peer, pl.ds(pl.multiple_of(chunk * CROWS, CROWS), CROWS), :],
            dst_ref=out_rest.at[pl.ds(pl.multiple_of(me * TH + chunk * CROWS, CROWS), CROWS), :],
            send_sem=out_send,
            recv_sem=out_recv,
            device_id={"tile": peer},
        )

    @pl.loop(0, CHUNKS)
    def _(chunk):
        @pl.loop(0, CROWS // 4)
        def _(part):
            for inner in range(4):
                row = chunk * CROWS + part * 4 + inner
                at = pl.ds(pl.multiple_of(row * frames, frames), frames)
                refit = dot_nt(new, shaped[row])
                flat[0, at, :] = cleaned[0, at, :] - refit[:, 0:128]
                flat[1, at, :] = cleaned[1, at, :] - refit[:, 128:256]

        @pl.loop(0, frames)
        def _(f):
            at = pl.ds(chunk * (CROWS * frames) + f, CROWS, stride=frames)
            rows = pl.ds(pl.multiple_of(chunk * CROWS, CROWS), CROWS)
            rest[f, rows, 0:128] = flat[0, at, :].astype(BF16)
            rest[f, rows, 128:256] = flat[1, at, :].astype(BF16)

        @pl.loop(1, tiles)
        def _(step):
            rest_copy(lax.rem(me + step, tiles), chunk).start()

    out_rest[pl.ds(pl.multiple_of(me * TH, TH), TH), :] = rest[me]

    for step in range(1, slabs):
        peer = lax.rem(slab + step, slabs)
        pltpu.make_async_copy(gathered.at[peer], gathered.at[peer], gram_recv.at[peer]).wait()
    whole = gathered[...].reshape(slabs * frames, KT)
    out_gram[...] = dot_tn(whole, whole)

    for step in range(1, slabs):
        gram_copy(lax.rem(slab + step, slabs)).wait_send()
    for g in range(groups):

        @pl.when(me > 0)
        def _():
            halo_up(g).wait_send()

        @pl.when(me < tiles - 1)
        def _():
            halo_down(g).wait_send()

    others = pl.ds(0, (tiles - 1) * TH)
    everything = out_rest.at[others, :]
    pltpu.make_async_copy(movie.at[0, others, :], movie.at[0, others, :], in_send).wait()
    pltpu.make_async_copy(everything, everything, out_send).wait()
    pltpu.make_async_copy(everything, everything, out_recv).wait()


def solution(mesh):
    tiles, slabs = mesh.shape["tile"], mesh.shape["frame"]
    frames = tiles
    group = min(8, frames)
    groups = frames // group

    def per_device(movie, footprints, support, traces, border_weight, border_offsets):
        vmem = pl.BlockSpec(memory_space=pltpu.VMEM)
        hbm = pl.BlockSpec(memory_space=pl.ANY)
        state, gram, rest = pl.pallas_call(
            functools.partial(kernel, tiles, slabs),
            out_shape=(
                jax.ShapeDtypeStruct((frames, KT), F32),
                jax.ShapeDtypeStruct((KT, KT), F32),
                jax.ShapeDtypeStruct((tiles * TH, W), BF16),
            ),
            in_specs=[hbm, hbm, vmem, vmem, vmem, vmem],
            out_specs=(vmem, vmem, vmem),
            scratch_shapes=[
                pltpu.VMEM((TH, W, KT), BF16),
                pltpu.VMEM((frames, TH, W), BF16),
                pltpu.VMEM((2, TH * frames, 128), F32),
                pltpu.VMEM((frames, TH, W), BF16),
                pltpu.VMEM((frames, HB, W), BF16),
                pltpu.VMEM((frames, HB, W), BF16),
                pltpu.VMEM((4 * W, W), BF16),
                pltpu.VMEM((4 * TH, 256), BF16),
                pltpu.VMEM((group * TH, 4 * W), BF16),
                pltpu.VMEM((2, TH * frames, 128), F32),
                pltpu.VMEM((KT, KT), F32),
                pltpu.VMEM((frames, TH, W), BF16),
                pltpu.VMEM((slabs, frames, KT), BF16),
                pltpu.SemaphoreType.DMA((NBLOCK,)),
                pltpu.SemaphoreType.DMA,
                pltpu.SemaphoreType.DMA((frames,)),
                pltpu.SemaphoreType.DMA((2, groups)),
                pltpu.SemaphoreType.DMA((2, groups)),
                pltpu.SemaphoreType.DMA((slabs,)),
                pltpu.SemaphoreType.DMA((slabs,)),
                pltpu.SemaphoreType.DMA,
                pltpu.SemaphoreType.DMA,
            ],
            compiler_params=pltpu.CompilerParams(
                collective_id=0, has_side_effects=True, vmem_limit_bytes=56 * 1024 * 1024
            ),
            name="alternation",
        )(movie, footprints, support, traces.T, border_weight, border_offsets.T)
        return state.T, gram, rest[None]

    return jax.shard_map(
        per_device,
        mesh=mesh,
        in_specs=(
            P(("frame", "tile"), None, None),
            P("tile", None, None),
            P("tile", None),
            P("tile", "frame"),
            P("tile", None),
            P(),
        ),
        out_specs=(P("tile", "frame"), P("tile", None), P(("frame", "tile"), None, None)),
        check_vma=False,
    )
```

```python
import functools
import math

import jax
import jax.numpy as jnp
import numpy as np
from jax import lax
from jax.experimental import pallas as pl
from jax.experimental.pallas import tpu as pltpu
from jax.sharding import PartitionSpec as P

RR = 16
GR = 4
BR = 8
SWEEPS = 3
NR = 64
TH = 64
W = 256
KT = 384
HB = 32
NBLOCK = TH // BR
CHUNKS = 4
CROWS = TH // CHUNKS
F32 = jnp.float32
BF16 = jnp.bfloat16

_raw = np.exp(-2.0 * np.arange(-GR, GR + 1, dtype=np.float32) ** 2 / np.float32(GR * GR)).astype(np.float32)
TAPS = _raw / _raw.sum(dtype=np.float32)


def tap(d):
    away = jnp.abs(d)
    value = jnp.zeros(d.shape, F32)
    for step in range(GR + 1):
        value = jnp.where(away == step, float(TAPS[GR + step]), value)
    return value


def dot(a, b):
    return jnp.dot(a, b, preferred_element_type=F32)


def dot_nt(a, b):
    return lax.dot_general(a, b, (((1,), (1,)), ((), ())), preferred_element_type=F32)


def dot_tn(a, b):
    return lax.dot_general(a, b, (((0,), (0,)), ((), ())), preferred_element_type=F32)


def split(a):
    high = a.astype(BF16)
    return high, (a - high.astype(F32)).astype(BF16)


def build_operators(me, tiles, offs, rmat, cmat):
    rows_of, cols_of = offs[0:1, :], offs[1:2, :]
    place = lax.broadcasted_iota(jnp.int32, (128, NR), 0) - RR
    col_hot = (place == cols_of).astype(F32)
    row_hot = (place == rows_of).astype(F32)
    inner = jnp.abs(rows_of) < RR
    which = lax.broadcasted_iota(jnp.int32, (8, NR), 0)
    side_rows = jnp.where(which == 0, rows_of, jnp.where(which == 1, rows_of, 99))
    is_row = ((which == 0) & (side_rows == -RR)) | ((which == 1) & (side_rows == RR))
    is_col = inner & (((which == 0) & (cols_of == -RR)) | ((which == 1) & (cols_of == RR)))
    row_sides = dot_nt(is_row.astype(F32), col_hot)
    col_sides = dot_nt(is_col.astype(F32), row_hot)

    u = lax.broadcasted_iota(jnp.int32, (W, W), 0)
    x = lax.broadcasted_iota(jnp.int32, (W, W), 1)
    gap = u - x
    smooth_high, smooth_low = split(tap(gap))
    for side in range(2):
        band = jnp.zeros((W, W), F32)
        for b in range(-RR, RR + 1):
            band = jnp.where(gap == b, row_sides[side : side + 1, b + RR : b + RR + 1], band)
        band = band.astype(BF16)
        cmat[side * W : (side + 1) * W, :] = (dot(smooth_high, band) + dot(smooth_low, band)).astype(BF16)
        shift = RR if side == 0 else -RR
        source = x - shift
        kept = (source >= 0) & (source < W)
        cmat[(2 + side) * W : (3 + side) * W, :] = jnp.where(kept, tap(u - source), 0.0).astype(BF16)

    total_rows = tiles * TH
    y = lax.broadcasted_iota(jnp.int32, (TH, 128), 0)
    v = lax.broadcasted_iota(jnp.int32, (TH, 128), 1)
    rel = jnp.where(v < TH, v, jnp.where(v < TH + HB, v - (TH + HB), v - HB))

    def inside(row):
        place_of = row + me * TH
        return (place_of >= 0) & (place_of < total_rows)

    seen = inside(rel)
    parts = []
    for a in (-RR, RR):
        parts.append(jnp.where(seen & inside(y + a), tap(rel - y - a), 0.0))
    left = jnp.zeros((TH, 128), F32)
    right = jnp.zeros((TH, 128), F32)
    for a in range(-RR + 1, RR):
        term = jnp.where(seen & inside(y + a), tap(rel - y - a), 0.0)
        left = left + term * col_sides[0:1, a + RR : a + RR + 1]
        right = right + term * col_sides[1:2, a + RR : a + RR + 1]
    for index, part in enumerate(parts + [left, right]):
        high, low = split(part)
        rmat[index * TH : (index + 1) * TH, 0:128] = high
        rmat[index * TH : (index + 1) * TH, 128:256] = low


def far_first(planes):
    def hops(distance, size):
        return min(distance, size - distance)

    every = [(dz, dy, dc) for dz in range(planes) for dy in range(4) for dc in range(2)]
    return sorted(every[1:], key=lambda o: -hops(o[0], planes) - hops(o[1], 4))


def kernel(
    tiles, slabs, movie, foot, support, traces, weight, offs, out_traces, out_gram, out_rest,
    shaped, strips, flat, first, above, below, cmat, rmat, stage, cleaned, coupling, rest, gathered,
    load_sem, in_send, in_recv, halo_send, halo_recv, gram_send, gram_recv, out_send, out_recv,
):
    me = lax.axis_index("tile")
    slab = lax.axis_index("frame")
    frames = tiles
    group = min(8, frames)
    groups = frames // group

    barrier = pltpu.get_barrier_semaphore()

    @pl.loop(1, tiles)
    def _(step):
        pl.semaphore_signal(barrier, inc=1, device_id={"tile": lax.rem(me + step, tiles)})

    for step in range(1, slabs):
        pl.semaphore_signal(barrier, inc=1, device_id={"frame": lax.rem(slab + step, slabs)})

    for block in range(NBLOCK):
        span = pl.ds(block * BR, BR)
        pltpu.make_async_copy(foot.at[span], shaped.at[span], load_sem.at[block]).start()

    pl.semaphore_wait(barrier, tiles - 1 + slabs - 1)

    plane, line, core = me // 8, (me // 2) % 4, me % 2
    planes = tiles // 8

    def peer_at(offset):
        dz, dy, dc = offset
        return lax.rem(plane + dz, planes) * 8 + lax.rem(line + dy, 4) * 2 + lax.rem(core + dc, 2)

    offsets = far_first(planes)

    def movie_copy(peer):
        return pltpu.make_async_remote_copy(
            src_ref=movie.at[0, pl.ds(pl.multiple_of(peer * TH, TH), TH), :],
            dst_ref=strips.at[me],
            send_sem=in_send,
            recv_sem=in_recv.at[me],
            device_id={"tile": peer},
        )

    for offset in offsets:
        movie_copy(peer_at(offset)).start()

    pltpu.make_async_copy(
        movie.at[0, pl.ds(pl.multiple_of(me * TH, TH), TH), :], strips.at[me], in_recv.at[me]
    ).start()

    @pl.when(me == 0)
    def _():
        above[...] = jnp.zeros(above.shape, BF16)

    @pl.when(me == tiles - 1)
    def _():
        below[...] = jnp.zeros(below.shape, BF16)

    build_operators(me, tiles, offs, rmat, cmat)

    coupling[...] = jnp.zeros(coupling.shape, F32)
    old = traces[...]

    @pl.loop(0, NBLOCK)
    def _(block):
        span = pl.ds(block * BR, BR)
        pltpu.make_async_copy(foot.at[span], shaped.at[span], load_sem.at[block]).wait()
        mask = support[pl.ds(block, 1), :].astype(F32).astype(BF16)
        for inner in range(BR):
            row = block * BR + inner
            masked = shaped[row] * mask
            shaped[row] = masked
            fit = dot_nt(old, masked)
            at = pl.ds(pl.multiple_of(row * frames, frames), frames)
            flat[0, at, :] = fit[:, 0:128]
            flat[1, at, :] = fit[:, 128:256]
        pixels = shaped[span].reshape(BR * W, KT)
        coupling[...] += dot_tn(pixels, pixels)

    def halo_up(g):
        span = pl.ds(g * group, group)
        return pltpu.make_async_remote_copy(
            src_ref=first.at[span, pl.ds(0, HB), :],
            dst_ref=below.at[span],
            send_sem=halo_send.at[0, g],
            recv_sem=halo_recv.at[0, g],
            device_id={"tile": lax.max(me - 1, 0)},
        )

    def halo_down(g):
        span = pl.ds(g * group, group)
        return pltpu.make_async_remote_copy(
            src_ref=first.at[span, pl.ds(TH - HB, HB), :],
            dst_ref=above.at[span],
            send_sem=halo_send.at[1, g],
            recv_sem=halo_recv.at[1, g],
            device_id={"tile": lax.min(me + 1, tiles - 1)},
        )

    steps = sorted(range(planes), key=lambda d: -min(d, planes - d))

    for dz in steps:
        g = lax.rem(plane + planes - dz, planes)

        @pl.loop(0, group)
        def _(inner):
            f = g * group + inner
            pltpu.make_async_copy(strips.at[f], strips.at[f], in_recv.at[f]).wait()
            seen = strips[f].astype(F32)
            at = pl.ds(f, TH, stride=frames)
            first[f, :, 0:128] = (seen[:, 0:128] - flat[0, at, :]).astype(BF16)
            first[f, :, 128:256] = (seen[:, 128:256] - flat[1, at, :]).astype(BF16)

        @pl.when(me > 0)
        def _():
            halo_up(g).start()

        @pl.when(me < tiles - 1)
        def _():
            halo_down(g).start()

    scale = weight[...] / math.sqrt(NR)
    for dz in steps:
        g = lax.rem(plane + planes - dz, planes)

        @pl.when(me > 0)
        def _():
            halo_down(g).wait_recv()

        @pl.when(me < tiles - 1)
        def _():
            halo_up(g).wait_recv()

        for inner in range(group):
            f = g * group + inner
            window = jnp.concatenate([first[f], above[f], below[f]], axis=0)
            filtered = dot(rmat[...], jnp.concatenate([window, window], axis=0))
            for side in range(4):
                stage[inner * TH : (inner + 1) * TH, side * W : (side + 1) * W] = filtered[
                    side * TH : (side + 1) * TH
                ].astype(BF16)

        ring = dot(stage[...], cmat[...])
        for inner in range(group):
            f = g * group + inner
            clean = strips[f].astype(F32) - scale * ring[inner * TH : (inner + 1) * TH]
            clean = clean.astype(BF16).astype(F32)
            at = pl.ds(f, TH, stride=frames)
            cleaned[0, at, :] = clean[:, 0:128]
            cleaned[1, at, :] = clean[:, 128:256]

    def project(row, total):
        at = pl.ds(pl.multiple_of(row * frames, frames), frames)
        pixels = jnp.concatenate([cleaned[0, at, :], cleaned[1, at, :]], axis=1).astype(BF16)
        return total + dot(pixels, shaped[row])

    def project_block(block, total):
        for inner in range(BR):
            total = project(block * BR + inner, total)
        return total

    projected = lax.fori_loop(0, NBLOCK, project_block, jnp.zeros((frames, KT), F32))

    matrix = coupling[...]
    here = lax.broadcasted_iota(jnp.int32, (KT, KT), 0) == lax.broadcasted_iota(jnp.int32, (KT, KT), 1)
    floor = jnp.maximum(jnp.sum(jnp.where(here, matrix, 0.0), axis=0, keepdims=True), 1.0)
    inverse = 1.0 / floor
    high, low = split(jnp.where(here, 1.0, 0.0) - matrix * inverse)
    step_matrix = jnp.concatenate([high, high, low], axis=0)
    drive = projected / floor
    state = old.astype(F32)
    for _ in range(SWEEPS):
        high, low = split(state)
        state = jnp.maximum(dot(jnp.concatenate([high, low, high], axis=1), step_matrix) + drive, 0.0)
    out_traces[...] = state
    new = state.astype(BF16)
    gathered[slab] = new

    def gram_copy(peer):
        return pltpu.make_async_remote_copy(
            src_ref=gathered.at[slab],
            dst_ref=gathered.at[slab],
            send_sem=gram_send.at[peer],
            recv_sem=gram_recv.at[slab],
            device_id={"frame": peer},
        )

    for step in range(1, slabs):
        gram_copy(lax.rem(slab + step, slabs)).start()

    def rest_copy(peer, chunk):
        return pltpu.make_async_remote_copy(
            src_ref=rest.at[peer, pl.ds(pl.multiple_of(chunk * CROWS, CROWS), CROWS), :],
            dst_ref=out_rest.at[pl.ds(pl.multiple_of(me * TH + chunk * CROWS, CROWS), CROWS), :],
            send_sem=out_send,
            recv_sem=out_recv,
            device_id={"tile": peer},
        )

    @pl.loop(0, CHUNKS)
    def _(chunk):
        @pl.loop(0, CROWS // 4)
        def _(part):
            for inner in range(4):
                row = chunk * CROWS + part * 4 + inner
                at = pl.ds(pl.multiple_of(row * frames, frames), frames)
                refit = dot_nt(new, shaped[row])
                flat[0, at, :] = cleaned[0, at, :] - refit[:, 0:128]
                flat[1, at, :] = cleaned[1, at, :] - refit[:, 128:256]

        @pl.loop(0, frames)
        def _(f):
            at = pl.ds(chunk * (CROWS * frames) + f, CROWS, stride=frames)
            rows = pl.ds(pl.multiple_of(chunk * CROWS, CROWS), CROWS)
            rest[f, rows, 0:128] = flat[0, at, :].astype(BF16)
            rest[f, rows, 128:256] = flat[1, at, :].astype(BF16)

        for offset in offsets:
            rest_copy(peer_at(offset), chunk).start()

    out_rest[pl.ds(pl.multiple_of(me * TH, TH), TH), :] = rest[me]

    for step in range(1, slabs):
        peer = lax.rem(slab + step, slabs)
        pltpu.make_async_copy(gathered.at[peer], gathered.at[peer], gram_recv.at[peer]).wait()
    whole = gathered[...].reshape(slabs * frames, KT)
    out_gram[...] = dot_tn(whole, whole)

    for step in range(1, slabs):
        gram_copy(lax.rem(slab + step, slabs)).wait_send()
    for g in range(groups):

        @pl.when(me > 0)
        def _():
            halo_up(g).wait_send()

        @pl.when(me < tiles - 1)
        def _():
            halo_down(g).wait_send()

    others = pl.ds(0, (tiles - 1) * TH)
    everything = out_rest.at[others, :]
    pltpu.make_async_copy(movie.at[0, others, :], movie.at[0, others, :], in_send).wait()
    pltpu.make_async_copy(everything, everything, out_send).wait()
    pltpu.make_async_copy(everything, everything, out_recv).wait()


def write_out(state, gram, rest, out_state, out_gram, out_rest, sems):
    pairs = ((rest, out_rest), (gram, out_gram), (state, out_state))
    copies = [pltpu.make_async_copy(a, b, sems.at[i]) for i, (a, b) in enumerate(pairs)]
    for copy in copies:
        copy.start()
    for copy in copies:
        copy.wait()


def solution(mesh):
    tiles, slabs = mesh.shape["tile"], mesh.shape["frame"]
    frames = tiles
    group = min(8, frames)
    groups = frames // group

    def per_device(movie, footprints, support, traces, border_weight, border_offsets):
        vmem = pl.BlockSpec(memory_space=pltpu.VMEM)
        hbm = pl.BlockSpec(memory_space=pl.ANY)
        state, gram, rest = pl.pallas_call(
            functools.partial(kernel, tiles, slabs),
            out_shape=(
                pltpu.VMEM((frames, KT), F32),
                pltpu.VMEM((KT, KT), F32),
                pltpu.VMEM((tiles * TH, W), BF16),
            ),
            in_specs=[hbm, hbm, vmem, vmem, vmem, vmem],
            out_specs=(vmem, vmem, vmem),
            scratch_shapes=[
                pltpu.VMEM((TH, W, KT), BF16),
                pltpu.VMEM((frames, TH, W), BF16),
                pltpu.VMEM((2, TH * frames, 128), F32),
                pltpu.VMEM((frames, TH, W), BF16),
                pltpu.VMEM((frames, HB, W), BF16),
                pltpu.VMEM((frames, HB, W), BF16),
                pltpu.VMEM((4 * W, W), BF16),
                pltpu.VMEM((4 * TH, 256), BF16),
                pltpu.VMEM((group * TH, 4 * W), BF16),
                pltpu.VMEM((2, TH * frames, 128), F32),
                pltpu.VMEM((KT, KT), F32),
                pltpu.VMEM((frames, TH, W), BF16),
                pltpu.VMEM((slabs, frames, KT), BF16),
                pltpu.SemaphoreType.DMA((NBLOCK,)),
                pltpu.SemaphoreType.DMA,
                pltpu.SemaphoreType.DMA((frames,)),
                pltpu.SemaphoreType.DMA((2, groups)),
                pltpu.SemaphoreType.DMA((2, groups)),
                pltpu.SemaphoreType.DMA((slabs,)),
                pltpu.SemaphoreType.DMA((slabs,)),
                pltpu.SemaphoreType.DMA,
                pltpu.SemaphoreType.DMA,
            ],
            compiler_params=pltpu.CompilerParams(
                collective_id=0, has_side_effects=True, vmem_limit_bytes=56 * 1024 * 1024
            ),
            name="alternation",
        )(movie, footprints, support, traces.T, border_weight, border_offsets.T)
        state, gram, rest = pl.pallas_call(
            write_out,
            out_shape=(
                jax.ShapeDtypeStruct(state.shape, F32),
                jax.ShapeDtypeStruct(gram.shape, F32),
                jax.ShapeDtypeStruct(rest.shape, BF16),
            ),
            in_specs=[vmem, vmem, vmem],
            out_specs=(hbm, hbm, hbm),
            scratch_shapes=[pltpu.SemaphoreType.DMA((3,))],
            name="write_out",
        )(*[pltpu.with_memory_space_constraint(r, pltpu.VMEM) for r in (state, gram, rest)])
        return state.T, gram, rest[None]

    return jax.shard_map(
        per_device,
        mesh=mesh,
        in_specs=(
            P(("frame", "tile"), None, None),
            P("tile", None, None),
            P("tile", None),
            P("tile", "frame"),
            P("tile", None),
            P(),
        ),
        out_specs=(P("tile", "frame"), P("tile", None), P(("frame", "tile"), None, None)),
        check_vma=False,
    )
```
